32 devices in a mesh: energy: 16 (over z, y, x), slab: 2 (over core).
Axes of the slice: x: 2, y: 2, z: 4, core: 2. Of those that a mesh axis runs over, the one named last changes fastest.
Arguments:
- hamiltonian: float32 [2, 128, 128], P('slab'), may hold values from -0.25 to 0.25
- sigma_real: float32 [16, 2, 128, 128], P('energy', 'slab'), may hold values from -0.625 to 0.625
- scatter_rate: float32 [16, 2, 128], P('energy', 'slab'), may hold values from 0.02 to 0.2
- broadening: float32 [16], P('energy'), may hold values from 0.02 to 0.1
- coupling: float32 [2, 128], P('slab'), may hold values from 0.8 to 1.2
- coupling_perm: int32 [2, 128], P('slab'), may hold values from 0 to 127, each once within a row
- mode_offset: int32 [6], replicated, may hold values from 1 to 4
- mode_weight: int32 [6], replicated, may hold values from 1 to 4
- occupation: float32 [6], replicated, may hold values from 0.1 to 3
Outputs:
- green_diag: float32 [16, 2, 2, 128, 128], P('energy', 'slab')
- sigma_new: float32 [16, 2, 2, 128, 128], P('energy', 'slab')
The draws below stay inside these ranges and needn't reach their ends.
Inputs may be any that keep to these rules, and one draw needn't show every extreme that they name: Each row of coupling_perm is a permutation of the 128 orbitals.
All inputs are finite; a program needn't handle non-finite values.
Results may differ from the reference program's by a relative error of at most 0.0003.
Values sent between devices are 32-bit elements; how exact they have to be, the bound alone decides.
A program may use at most 64 MiB of HBM per device.

```python
import math
import jax
import jax.numpy as jnp
from jax import lax

N = 128
MODES = 6
ENERGIES = 16
SLABS = 2


def touch_ends(entries, stream_key, low, largest):
    dims = entries.shape
    place = [jax.random.randint(jax.random.fold_in(stream_key, axis), (), 0, dims[axis]) for axis in range(len(dims))]
    entries = entries.at[tuple(place)].set(low)
    longest = dims.index(max(dims))
    place[longest] = (place[longest] + 1) % dims[longest]
    return entries.at[tuple(place)].set(largest)


def levels(own_key, extent, pieces, low, largest):
    def one(dim, parts):
        steps = jax.random.uniform(jax.random.fold_in(jax.random.fold_in(own_key, 6), dim), (parts,), jnp.float32, low / len(pieces), largest / len(pieces))
        return jnp.repeat(jnp.exp(steps), extent[dim] // parts).reshape((-1,) + (1,) * (len(extent) - dim - 1))

    factor_of = one(*pieces[0])
    for cut in pieces[1:]:
        factor_of = factor_of * one(*cut)
    return factor_of


def normal_values(stream_key, shape, deviation, limit, cuts=(), held_as=jnp.bfloat16):
    array = deviation * jax.random.normal(stream_key, shape, jnp.float32)
    if cuts:
        array = array * levels(stream_key, shape, cuts, -0.22, 0.18)
    return jnp.clip(array, -limit, limit).astype(held_as)


def setup_inputs(seed: int = 0) -> dict:
    seeds = jax.random.split(jax.random.key(seed), 10)
    hamiltonian = normal_values(seeds[0], (SLABS, N, N), (4 * N) ** -0.5, 0.25, ((0, 2),), jnp.float32)
    sigma_real = normal_values(seeds[1], (ENERGIES, SLABS, N, N), 0.04, 0.625, ((0, 16), (1, 2)), jnp.float32)
    scatter_rate = jnp.clip(jnp.exp(math.log(0.2) - 2.3025851 * jax.random.uniform(seeds[2], (ENERGIES, SLABS, N), jnp.float32) ** levels(seeds[2], (ENERGIES, SLABS, N), ((0, 16), (1, 2)), -0.2, 0.2)), 0.02, 0.2)
    broadening = jnp.clip(jnp.exp(math.log(0.1) - 1.609438 * jax.random.uniform(seeds[3], (ENERGIES,), jnp.float32) ** levels(seeds[3], (ENERGIES,), ((0, 16),), -0.2, 0.2)), 0.02, 0.1)
    coupling = jnp.clip(0.8 + 0.40000004 * jax.random.uniform(seeds[4], (SLABS, N), jnp.float32) ** levels(seeds[4], (SLABS, N), ((0, 2),), -0.2, 0.2), 0.8, 1.2)
    coupling_perm = jax.vmap(lambda own: jax.random.permutation(own, N))(jax.random.split(seeds[5], SLABS)).reshape((SLABS, N)).astype(jnp.int32)
    mode_offset = touch_ends(jax.random.randint(seeds[6], (MODES,), 1, ENERGIES // 4 + 1), jax.random.fold_in(seeds[6], 1), 1, (ENERGIES // 4 + 1) - 1).astype(jnp.int32)
    mode_weight = touch_ends(jax.random.randint(seeds[7], (MODES,), 1, 5), jax.random.fold_in(seeds[7], 1), 1, 4).astype(jnp.int32)
    occupation = jnp.clip(jnp.exp(jax.random.uniform(seeds[8], (MODES,), jnp.float32, math.log(0.1), math.log(3.0))), 0.1, 3.0)
    return dict(hamiltonian=hamiltonian, sigma_real=sigma_real, scatter_rate=scatter_rate, broadening=broadening, coupling=coupling, coupling_perm=coupling_perm, mode_offset=mode_offset, mode_weight=mode_weight, occupation=occupation)


exact_dots = lax.Precision.HIGHEST
phonon_scale = 0.01

def left_apply(matrix, block):
    return jnp.einsum('ij,ecjk->ecik', matrix, block, precision=exact_dots)

def right_apply(block, matrix):
    return jnp.einsum('ecij,jk->ecik', block, matrix, precision=exact_dots)

def inward(coupled, block):
    return left_apply(coupled.T, right_apply(block, coupled))

def outward(coupled, block):
    return left_apply(coupled, right_apply(block, coupled.T))

def complex_inverse(block):
    real_part = block[:, 0]
    imag_part = block[:, 1]
    width = real_part.shape[-1]
    upper = jnp.concatenate([real_part, -imag_part], -1)
    lower_rows = jnp.concatenate([imag_part, real_part], -1)
    stacked = jnp.concatenate([upper, lower_rows], -2)
    target = jnp.concatenate([jnp.eye(width, dtype=jnp.float32), jnp.zeros((width, width), jnp.float32)], 0)
    target = jnp.broadcast_to(target, stacked.shape[:-2] + target.shape)
    solved = jnp.linalg.solve(stacked, target)
    return jnp.stack([solved[:, :width], solved[:, width:]], 1)

def lorentz(offset, total):
    return 1.0 / (1.0 + (16.0 * offset / total) ** 2)

def kernel_rows(row_energy, col_energy, offsets, weights, occupied, total):
    spread = col_energy[None, :, None] - row_energy[:, None, None]
    shifts = offsets.astype(jnp.float32)
    strength = weights.astype(jnp.float32)
    terms = strength * (occupied + 1.0) * lorentz(spread - shifts, total) + strength * occupied * lorentz(spread + shifts, total)
    return jnp.sum(terms, -1) / offsets.shape[0]

def reference(hamiltonian, sigma_real, scatter_rate, broadening, coupling, coupling_perm, mode_offset, mode_weight, occupation):
    identity_matrix = jnp.eye(N, dtype=jnp.float32)
    grid_index = jnp.arange(ENERGIES, dtype=jnp.float32)
    energy = -2.0 + 4.0 * grid_index / (ENERGIES - 1)
    columns = jnp.arange(N, dtype=jnp.int32)
    blocks = []
    couplings = []
    for slab_num in range(SLABS):
        symmetric = 0.5 * (hamiltonian[slab_num] + hamiltonian[slab_num].T)
        real_self = sigma_real[:, slab_num]
        real_self = 0.5 * (real_self + jnp.swapaxes(real_self, -1, -2))
        damping = broadening[:, None] + scatter_rate[:, slab_num]
        if slab_num == 0:
            damping = damping + coupling[0][None, :] ** 2
        real_block = energy[:, None, None] * identity_matrix - symmetric - real_self
        imag_block = damping[:, :, None] * identity_matrix
        blocks.append(jnp.stack([real_block, imag_block], 1))
        couplings.append(coupling[slab_num][:, None] * (coupling_perm[slab_num][:, None] == columns[None, :]).astype(jnp.float32))
    from_left = [jnp.zeros_like(blocks[0])]
    left_green = complex_inverse(blocks[0])
    for slab_num in range(1, SLABS):
        from_left.append(inward(couplings[slab_num], left_green))
        if slab_num < SLABS - 1:
            left_green = complex_inverse(blocks[slab_num] - from_left[slab_num])
    from_right = [jnp.zeros_like(blocks[0]) for slab_num in range(SLABS)]
    right_green = complex_inverse(blocks[SLABS - 1])
    for slab_num in range(SLABS - 2, -1, -1):
        from_right[slab_num] = outward(couplings[slab_num + 1], right_green)
        if slab_num > 0:
            right_green = complex_inverse(blocks[slab_num] - from_right[slab_num])
    green_diag = jnp.stack([complex_inverse(blocks[slab_num] - from_left[slab_num] - from_right[slab_num]) for slab_num in range(SLABS)], 1)
    kernel = kernel_rows(grid_index, grid_index, mode_offset, mode_weight, occupation, float(ENERGIES))
    sigma_new = phonon_scale * jnp.einsum('ef,fsckl->esckl', kernel, green_diag, precision=exact_dots)
    return (green_diag, sigma_new)
```

```python
import functools

import jax
import jax.numpy as jnp
from jax import lax
from jax.experimental import pallas as pl
from jax.experimental.pallas import tpu as pltpu
from jax.sharding import PartitionSpec as P

exact_dots = lax.Precision.HIGHEST
phonon_scale = 0.01
panel_rows = 16
panel_columns = 8
kernel_bytes = 8 * 2**20
VMEM = pl.BlockSpec(memory_space=pltpu.VMEM)
MESH = pl.DeviceIdType.MESH
SMEM = pl.BlockSpec(memory_space=pltpu.SMEM)


def iota(shape, dim):
    return lax.broadcasted_iota(jnp.int32, shape, dim)


def three_parts(value):
    high = value.astype(jnp.bfloat16)
    rest = value - high.astype(jnp.float32)
    middle = rest.astype(jnp.bfloat16)
    low = (rest - middle.astype(jnp.float32)).astype(jnp.bfloat16)
    return high, middle, low


def bf16_dot(former, latter, contract):
    return lax.dot_general(
        former, latter, (contract, ((), ())), preferred_element_type=jnp.float32
    )


def sweep_panel(real, imag, first):
    shape = real.shape
    lanes, rows = iota(shape, 1), iota(shape, 0)
    for start in range(0, shape[0], panel_columns):
        pivots = range(start, start + panel_columns)
        cols = {
            k: [jnp.broadcast_to(part[:, first + k : first + k + 1], shape) for part in (real, imag)]
            for k in pivots
        }
        for k in pivots:
            col_real, col_imag = cols[k]
            pivot_real, pivot_imag = col_real[k : k + 1], col_imag[k : k + 1]
            scale = 1.0 / (pivot_real * pivot_real + pivot_imag * pivot_imag)
            inv_real, inv_imag = pivot_real * scale, -pivot_imag * scale
            here, mine = lanes == first + k, rows == k
            real = jnp.where(here, jnp.where(mine, 1.0, 0.0), real)
            imag = jnp.where(here, 0.0, imag)

            def step(part_real, part_imag):
                row_real, row_imag = part_real[k : k + 1], part_imag[k : k + 1]
                new_real = row_real * inv_real - row_imag * inv_imag
                new_imag = row_real * inv_imag + row_imag * inv_real
                left_real = part_real - (col_real * new_real - col_imag * new_imag)
                left_imag = part_imag - (col_real * new_imag + col_imag * new_real)
                return jnp.where(mine, new_real, left_real), jnp.where(mine, new_imag, left_imag)

            for later in range(k + 1, start + panel_columns):
                cols[later] = step(*cols[later])
            real, imag = step(real, imag)
    return real, imag


def six_products(former, latter):
    former = [former[i] for i in (0, 0, 1, 1, 0, 2)]
    latter = [latter[i] for i in (0, 1, 0, 1, 2, 0)]
    return jnp.concatenate(former, 0), jnp.concatenate(latter, 0)


def sweep_inverse(real, imag, between=()):
    width = real.shape[-1]
    count = panel_rows
    firsts = range(0, width, count)
    parts = {at: [real[at : at + count], imag[at : at + count]] for at in firsts}
    for number, first in enumerate(firsts):
        old_real, old_imag = parts[first]
        real, imag = sweep_panel(old_real, old_imag, first)
        lanes = iota(real.shape, 1)
        inside = (lanes >= first) & (lanes < first + count)
        unit = jnp.where(lanes == iota(real.shape, 0) + first, 1.0, 0.0)
        side_real = three_parts(jnp.where(inside, unit - real, real))
        side_imag = three_parts(jnp.where(inside, -imag, imag))
        sides = [
            jnp.concatenate([jnp.concatenate([r, i], 1), jnp.concatenate([-i, r], 1)], 0)
            for r, i in zip(side_real, side_imag)
        ]
        olds = three_parts(jnp.concatenate([old_real, old_imag], 0))
        change = bf16_dot(*six_products(olds, sides), ((0,), (0,)))
        for at in firsts:
            if at != first:
                rows = slice(at, at + count)
                parts[at] = [
                    parts[at][0] - change[rows, :width],
                    parts[at][1] - change[rows, width:],
                ]
        parts[first] = [jnp.where(inside, -real, real), jnp.where(inside, -imag, imag)]
        if number in between:
            between[number]()
    return [jnp.concatenate([parts[at][c] for at in firsts], 0) for c in range(2)]


def column_of(row, unit):
    return jnp.sum(jnp.where(unit, row, 0.0), 1, keepdims=True)


def moved(real, imag, places, turned):
    rows = real.shape[0]
    both = jnp.concatenate(three_parts(jnp.concatenate([real, imag], 0)), 1)
    both = bf16_dot(both, jnp.concatenate([places] * 3, 0), ((1,), (0,)))
    both = jnp.concatenate([both[:rows], both[rows:]], 1)
    both = jnp.concatenate(three_parts(both), 0)
    both = bf16_dot(jnp.concatenate([turned] * 3, 1), both, ((1,), (0,)))
    return both[:, :rows], both[:, rows:]


def form_block(ham, sigma, rate, broad, coupling, slab, energy):
    width = ham.shape[-1]
    unit = iota((width, width), 0) == iota((width, width), 1)
    total = ham + sigma
    real = jnp.where(unit, energy, 0.0) - 0.5 * (total + total.T)
    return real, broad + rate + jnp.where(slab == 0, coupling * coupling, 0.0)


def pair_maps(row, perm, slab):
    width = row.shape[-1]
    rows, lanes = iota((width, width), 0), iota((width, width), 1)
    unit = rows == lanes
    by_column = rows.astype(jnp.float32) == perm
    by_row = lanes.astype(jnp.float32) == column_of(perm, unit)
    col = column_of(row, ((slab == 1) & by_column) | ((slab == 0) & unit))
    scale = col * jnp.sum(jnp.where(unit, col, 0.0), 0, keepdims=True)
    places = jnp.where(((slab == 1) & by_column) | ((slab == 0) & by_row), 1.0, 0.0)
    turned = jnp.where(((slab == 1) & by_row) | ((slab == 0) & by_column), 1.0, 0.0)
    return scale, places.astype(jnp.bfloat16), turned.astype(jnp.bfloat16)


def energy_of(total):
    return -2.0 + 4.0 * lax.axis_index("energy").astype(jnp.float32) / (total - 1)


def splat_kernel(splats, offsets, weights, occupied, total):
    shape = splats.shape[1:]
    spread = (iota(shape, 1) - (total - 1)).astype(jnp.float32)
    modes = offsets.shape[0]
    value = jnp.zeros(shape, jnp.float32)
    for mode in range(modes):
        shift = offsets[mode].astype(jnp.float32)
        strength = weights[mode].astype(jnp.float32)
        value += strength * (occupied[mode] + 1.0) * lorentz(spread - shift, float(total))
        value += strength * occupied[mode] * lorentz(spread + shift, float(total))
    value = value * (-phonon_scale / modes)
    for i in range(splats.shape[0]):
        splats[i] = jnp.broadcast_to(value[:, i : i + 1], shape)


def packed_rows(part):
    half = part.shape[0] // 2
    lanes, rows = iota((half, 2 * half), 1), iota((half, 2 * half), 0)
    lower = part[half:]
    packed = jnp.where(lanes < rows, pltpu.roll(lower, half, 1), part[:half])
    return packed, jnp.sum(jnp.where(lanes == rows + half, lower, 0.0), 0, keepdims=True)


def unpacked(packed, diagonal):
    half = packed.shape[0]
    lanes, rows = iota(packed.shape, 1), iota(packed.shape, 0)
    turned = jnp.concatenate([packed, jnp.zeros_like(packed)], 0).T
    upper = jnp.where(lanes >= rows, packed, turned[:half])
    corner = pltpu.roll(jnp.where(lanes < rows, packed, turned[:half]), half, 1)
    corner = jnp.where(lanes == rows + half, diagonal, corner)
    return upper, jnp.where(lanes < half, turned[half:], corner)


def pair_kernel(
    total,
    *refs,
):
    inputs, broad, green, fresh = refs[:8], *refs[8:11]
    pair_step_on_device(total, inputs, refs[11:19], broad, green, fresh, *refs[19:])


def pair_step_on_device(
    total,
    inputs,
    held,
    broad,
    green,
    fresh,
    input_sems,
    raw,
    theirs,
    scale,
    places,
    turned,
    negated,
    given,
    packed,
    rest,
    landed,
    rests,
    mixed,
    home,
    splats,
    pair_sems,
    away_sems,
    rest_sems,
    back_sems,
):
    fetches = [
        pltpu.make_async_copy(source, target, input_sems.at[i])
        for i, (source, target) in enumerate(zip(inputs, held))
    ]
    for fetch in fetches:
        fetch.start()
    ham, sigma, rate, coupling, perm, offsets, weights, occupied = held
    slab, me = lax.axis_index("slab"), lax.axis_index("energy")
    width = ham.shape[-1]
    half = width // 2
    rows = landed.shape[2]
    owner = slab == 1

    def across(step):
        peer = me
        bit = 1
        while bit < total:
            if step & bit:
                peer += jnp.where(lax.rem(me // bit, 2) == 0, bit, -bit)
            bit *= 2
        return peer

    peers = [across(step) for step in range(total)]
    barrier = pltpu.get_barrier_semaphore()

    def greet(step, core):
        target = {"energy": peers[step], "slab": core}
        pl.semaphore_signal(barrier, inc=1, device_id=target, device_id_type=MESH)

    for step in range(1, total):
        greet(step, 1)

    @pl.when(slab == 0)
    def _():
        greet(0, 1)

    @pl.when(owner)
    def _():
        for step in range(total):
            greet(step, 0)

    for fetch in fetches:
        fetch.wait()
    real, damping = form_block(
        ham[0], sigma[0, 0], rate[0], broad[0], coupling[...], slab, energy_of(total)
    )
    raw[:width] = real
    row = iota((8, width), 0)
    raw[width:] = jnp.where(
        row == 0, damping, jnp.where(row == 1, coupling[...], perm[...].astype(jnp.float32))
    )
    partner = {"slab": 1 - slab}
    swap = pltpu.make_async_remote_copy(
        raw, theirs, pair_sems.at[0], pair_sems.at[1], partner, MESH
    )

    def open_swap():
        @pl.when(slab == 0)
        def _():
            pl.semaphore_wait(barrier, total)

        @pl.when(owner)
        def _():
            pl.semaphore_wait(barrier, 2 * total - 1)

        swap.start()

    def close_swap():
        swap.wait_recv()
        row, order = (
            jnp.where(owner, raw[width + i : width + i + 1], theirs[width + i : width + i + 1])
            for i in (1, 2)
        )
        scale[...], places[...], turned[...] = pair_maps(row, order, slab)

    unit = iota((width, width), 0) == iota((width, width), 1)
    splat_kernel(splats, offsets, weights, occupied, total)
    real, imag = sweep_inverse(
        real, jnp.where(unit, damping, 0.0), {2: open_swap, 6: close_swap}
    )
    real, imag = moved(real * scale[...], imag * scale[...], places[...], turned[...])
    real, imag = sweep_inverse(
        theirs[:width] + real, jnp.where(unit, theirs[width : width + 1], 0.0) + imag
    )

    spare = []
    for part, value in enumerate((real, imag)):
        packed[part * half : (part + 1) * half], diagonal = packed_rows(value)
        spare.append(diagonal)
    rest[...] = spare[0] + pltpu.roll(jnp.broadcast_to(spare[1], (8, width)), half, 1)[:1]
    negated[0] = -real
    negated[1] = -imag

    def away(step):
        return pltpu.make_async_remote_copy(
            packed.at[pl.ds(peers[step] * rows, rows)],
            landed.at[slab, me],
            away_sems.at[0],
            away_sems.at[1],
            {"energy": peers[step], "slab": 1},
            MESH,
        )

    def rest_away(step):
        return pltpu.make_async_remote_copy(
            rest,
            rests.at[me],
            rest_sems.at[0],
            rest_sems.at[1],
            {"energy": peers[step], "slab": 1 - slab},
            MESH,
        )

    hand = pltpu.make_async_remote_copy(
        negated, given, pair_sems.at[2], pair_sems.at[3], partner, MESH
    )

    def back(e, part):
        return pltpu.make_async_remote_copy(
            mixed.at[part, e],
            home.at[pl.ds(me * rows, rows)],
            back_sems.at[0],
            back_sems.at[1],
            {"energy": e, "slab": 1 - part},
            MESH,
        )

    def whole(ref, count, sems):
        part = ref.at[pl.ds(0, count)]
        return pltpu.make_async_remote_copy(part, part, sems.at[0], sems.at[1], partner, MESH)

    own_rows = pl.ds(pl.multiple_of(me * rows, rows), rows)
    for step in range(total - 1, 0, -1):
        away(step).start()

    @pl.when(slab == 0)
    def _():
        away(0).start()

    hand.start()
    for step in range(total - 1, -1, -1):
        rest_away(step).start()

    @pl.when(owner)
    def _():
        landed[slab, me] = packed[own_rows, :]
        flat = (2 * total - 1) * rows
        wide = mixed.reshape(2 * total * rows, width)
        whole(wide, flat, away_sems).wait_recv()
        every = [landed[part] for part in range(2)]
        for e in range(total):
            factors = splats[total - 1 - e : 2 * total - 1 - e]
            for part in range(1, -1, -1):
                mixed[part, e] = jnp.sum(factors * every[part], 0)
            back(e, 1).start()

            @pl.when(me != e)
            def _():
                back(e, 0).start()

        home[own_rows, :] = mixed[0, me]

    hand.wait_recv()
    green[...] = given[...].reshape(2 * width, width)
    rest_all = pltpu.make_async_remote_copy(
        rests, rests, rest_sems.at[0], rest_sems.at[1], partner, MESH
    )
    rest_all.wait_recv()
    spare = jnp.zeros((1, width), jnp.float32)
    for f in range(total):
        spare += splats[f - me + total - 1, :1, :] * rests[f]
    fresh[width:] = jnp.broadcast_to(spare, (8, width))
    swap.wait_send()
    hand.wait_send()
    rest_all.wait_send()

    @pl.when(slab == 0)
    def _():
        whole(packed, width, away_sems).wait_send()
        whole(home, width, back_sems).wait_recv()

    @pl.when(owner)
    def _():
        whole(packed, width - rows, away_sems).wait_send()
        whole(home, width - rows, back_sems).wait_recv()
        flat = (2 * total - 1) * rows
        wide = mixed.reshape(2 * total * rows, width)
        whole(wide, flat, back_sems).wait_send()

    fresh[:width] = home[...]


def closing_kernel(green, fresh, green_out, fresh_out, unfolded, sems):
    width = fresh.shape[-1]
    half = width // 2
    first = pltpu.make_async_copy(green, green_out, sems.at[0])
    first.start()
    spare = fresh[width : width + 1]
    spare = [spare, pltpu.roll(jnp.broadcast_to(spare, (8, width)), half, 1)[:1]]
    for part in range(2):
        upper, lower = unpacked(fresh[part * half : (part + 1) * half, :], spare[part])
        unfolded[part * width : part * width + half, :] = upper
        unfolded[part * width + half : (part + 1) * width, :] = lower
    second = pltpu.make_async_copy(unfolded, fresh_out, sems.at[1])
    second.start()
    first.wait()
    second.wait()


def inverse_kernel(block, out):
    real, imag = sweep_inverse(block[0, 0], block[0, 1])
    out[0, 0] = -real
    out[0, 1] = -imag


def complex_inverse(block):
    count, _, width, _ = block.shape
    spec = pl.BlockSpec((1, 2, width, width), lambda i: (i, 0, 0, 0))
    return pl.pallas_call(
        inverse_kernel,
        grid=(count,),
        out_shape=jax.ShapeDtypeStruct(block.shape, jnp.float32),
        in_specs=[spec],
        out_specs=spec,
    )(block)


def passed_along(block, axis, distance):
    devices = range(lax.axis_size(axis))
    route = [(i - distance, i) for i in devices if i - distance in devices]
    return lax.ppermute(block, axis, route)


def left_apply(matrix, block):
    return jnp.einsum("ij,ecjk->ecik", matrix, block, precision=exact_dots)


def right_apply(block, matrix):
    return jnp.einsum("ecij,jk->ecik", block, matrix, precision=exact_dots)


def inward(coupled, block):
    return left_apply(coupled.T, right_apply(block, coupled))


def outward(coupled, block):
    return left_apply(coupled, right_apply(block, coupled.T))


def paired_inverse(first, second):
    count = first.shape[0]
    both = complex_inverse(jnp.concatenate([first, second], 0))
    return (both[:count], both[count:])


def lorentz(offset, total):
    return 1.0 / (1.0 + (16.0 * offset / total) ** 2)


def kernel_rows(row_energy, col_energy, offsets, weights, occupied, total):
    spread = col_energy[None, :, None] - row_energy[:, None, None]
    shifts = offsets.astype(jnp.float32)
    strength = weights.astype(jnp.float32)
    terms = strength * (occupied + 1.0) * lorentz(
        spread - shifts, total
    ) + strength * occupied * lorentz(spread + shifts, total)
    return jnp.sum(terms, -1) / offsets.shape[0]


def swept_green(hamiltonian, sigma_real, scatter_rate, broadening, coupling, coupling_perm):
    energy_count = broadening.shape[0]
    width = hamiltonian.shape[-1]
    slab_count = lax.axis_size("slab")
    total = energy_count * lax.axis_size("energy")
    slab_pos = lax.axis_index("slab")
    energy_ids = lax.axis_index("energy") * energy_count + jnp.arange(energy_count, dtype=jnp.int32)
    energy = -2.0 + 4.0 * energy_ids.astype(jnp.float32) / (total - 1)
    identity_matrix = jnp.eye(width, dtype=jnp.float32)
    symmetric = 0.5 * (hamiltonian[0] + hamiltonian[0].T)
    real_self = sigma_real[:, 0]
    real_self = 0.5 * (real_self + jnp.swapaxes(real_self, -1, -2))
    lead_rate = jnp.where(slab_pos == 0, coupling[0] ** 2, 0.0)
    damping = broadening[:, None] + scatter_rate[:, 0] + lead_rate[None, :]
    real_block = energy[:, None, None] * identity_matrix - symmetric - real_self
    imag_block = damping[:, :, None] * identity_matrix
    blocks = jnp.stack([real_block, imag_block], 1)
    columns = jnp.arange(width, dtype=jnp.int32)
    coupled = coupling[0][:, None] * (coupling_perm[0][:, None] == columns[None, :]).astype(
        jnp.float32
    )
    left_green = right_green = complex_inverse(blocks)
    from_left = jnp.zeros_like(blocks)
    from_right = jnp.zeros_like(blocks)
    for sweep_num in range(slab_count - 1):
        received = passed_along(left_green, "slab", 1)
        from_right = passed_along(outward(coupled, right_green), "slab", -1)
        from_left = inward(coupled, received)
        if sweep_num < slab_count - 2:
            left_green, right_green = paired_inverse(blocks - from_left, blocks - from_right)
    return complex_inverse(blocks - from_left - from_right)


def pair_step(
    hamiltonian,
    sigma_real,
    scatter_rate,
    broadening,
    coupling,
    coupling_perm,
    mode_offset,
    mode_weight,
    occupation,
):
    width = hamiltonian.shape[-1]
    total = lax.axis_size("energy")
    rows = width // total
    flat = jax.ShapeDtypeStruct((2 * width, width), jnp.float32)
    folded = jax.ShapeDtypeStruct((width + 8, width), jnp.float32)
    complex_block = pltpu.VMEM((2, width, width), jnp.float32)
    with_rows = pltpu.VMEM((width + 8, width), jnp.float32)
    square = pltpu.VMEM((width, width), jnp.float32)
    small_square = pltpu.VMEM((width, width), jnp.bfloat16)
    dma = pltpu.SemaphoreType.DMA
    arrays = (
        hamiltonian,
        sigma_real,
        scatter_rate[0],
        coupling,
        coupling_perm,
        mode_offset,
        mode_weight,
        occupation,
    )
    green, fresh = pl.pallas_call(
        functools.partial(pair_kernel, total),
        out_shape=(flat, folded),
        in_specs=[pl.BlockSpec(memory_space=pl.ANY)] * 8 + [SMEM],
        out_specs=(VMEM, VMEM),
        scratch_shapes=[pltpu.VMEM(array.shape, array.dtype) for array in arrays[:5]]
        + [pltpu.SMEM(array.shape, array.dtype) for array in arrays[5:]]
        + [
            dma((8,)),
            with_rows,
            with_rows,
            square,
            small_square,
            small_square,
            complex_block,
            complex_block,
            square,
            pltpu.VMEM((1, width), jnp.float32),
            pltpu.VMEM((2, total, rows, width), jnp.float32),
            pltpu.VMEM((total, 1, width), jnp.float32),
            pltpu.VMEM((2, total, rows, width), jnp.float32),
            square,
            pltpu.VMEM((2 * total - 1, 8, width), jnp.float32),
            dma((4,)),
            dma((2,)),
            dma((2,)),
            dma((2,)),
        ],
        compiler_params=pltpu.CompilerParams(
            collective_id=0, has_side_effects=True, vmem_limit_bytes=kernel_bytes
        ),
    )(*[pltpu.with_memory_space_constraint(array, pltpu.HBM) for array in arrays], broadening)
    anywhere = pl.BlockSpec(memory_space=pl.ANY)
    green, fresh = pl.pallas_call(
        closing_kernel,
        out_shape=(flat, flat),
        in_specs=[VMEM, VMEM],
        out_specs=(anywhere, anywhere),
        scratch_shapes=[pltpu.VMEM((2 * width, width), jnp.float32), dma((2,))],
        compiler_params=pltpu.CompilerParams(vmem_limit_bytes=kernel_bytes),
    )(green, fresh)
    shape = (1, 1, 2, width, width)
    return green.reshape(shape), fresh.reshape(shape)


def shards(
    hamiltonian,
    sigma_real,
    scatter_rate,
    broadening,
    coupling,
    coupling_perm,
    mode_offset,
    mode_weight,
    occupation,
):
    energy_count = broadening.shape[0]
    width = hamiltonian.shape[-1]
    total = energy_count * lax.axis_size("energy")
    grouped = total & (total - 1) == 0 and width == 8 * total
    if lax.axis_size("slab") == 2 and energy_count == 1 and grouped:
        return pair_step(
            hamiltonian,
            sigma_real,
            scatter_rate,
            broadening,
            coupling,
            coupling_perm,
            mode_offset,
            mode_weight,
            occupation,
        )
    green_diag = swept_green(
        hamiltonian, sigma_real, scatter_rate, broadening, coupling, coupling_perm
    )
    whole_grid = jnp.arange(total, dtype=jnp.float32)
    full_kernel = kernel_rows(
        whole_grid, whole_grid, mode_offset, mode_weight, occupation, float(total)
    )
    flat_rows = green_diag.reshape(energy_count, 2 * width, width)
    mixed = jnp.einsum(
        "ef,frc->erc",
        full_kernel,
        lax.all_to_all(flat_rows, "energy", split_axis=1, concat_axis=0, tiled=True),
        precision=exact_dots,
    )
    summed = lax.all_to_all(mixed, "energy", split_axis=0, concat_axis=1, tiled=True)
    summed = summed.reshape(energy_count, 2, width, width)
    sigma_new = phonon_scale * summed
    return (green_diag[:, None], sigma_new[:, None])


def solution(mesh):
    in_specs = (
        P("slab", None, None),
        P("energy", "slab", None, None),
        P("energy", "slab", None),
        P("energy"),
        P("slab", None),
        P("slab", None),
        P(),
        P(),
        P(),
    )
    out_specs = (P("energy", "slab", None, None, None), P("energy", "slab", None, None, None))
    return jax.shard_map(shards, mesh=mesh, in_specs=in_specs, out_specs=out_specs, check_vma=False)
```

```python
import functools

import jax
import jax.numpy as jnp
from jax import lax
from jax.experimental import pallas as pl
from jax.experimental.pallas import tpu as pltpu
from jax.sharding import PartitionSpec as P

exact_dots = lax.Precision.HIGHEST
phonon_scale = 0.01
group = 8
groups_ahead = 1
kernel_bytes = 8 * 2**20
VMEM = pl.BlockSpec(memory_space=pltpu.VMEM)
MESH = pl.DeviceIdType.MESH
SMEM = pl.BlockSpec(memory_space=pltpu.SMEM)


def iota(shape, dim):
    return lax.broadcasted_iota(jnp.int32, shape, dim)


def three_parts(value):
    high = value.astype(jnp.bfloat16)
    rest = value - high.astype(jnp.float32)
    middle = rest.astype(jnp.bfloat16)
    low = (rest - middle.astype(jnp.float32)).astype(jnp.bfloat16)
    return high, middle, low


def bf16_dot(former, latter, contract):
    return lax.dot_general(
        former, latter, (contract, ((), ())), preferred_element_type=jnp.float32
    )


def spread(part, lane):
    return jnp.broadcast_to(part[:, lane : lane + 1], part.shape)


def columns(block, first, count):
    return [[spread(part, first + k) for part in block] for k in range(count)]


def tree_sum(terms):
    while len(terms) > 1:
        terms = [a + b for a, b in zip(terms[::2], terms[1::2])]
    return terms[0]


def take_away(block, cols, rows):
    reals, imags = [], []
    for k, (col_real, col_imag) in enumerate(cols):
        row_real, row_imag = rows[0][k : k + 1], rows[1][k : k + 1]
        reals.append(col_real * row_real - col_imag * row_imag)
        imags.append(col_real * row_imag + col_imag * row_real)
    return [block[0] - tree_sum(reals), block[1] - tree_sum(imags)]


def sweep_group(block, first):
    real, imag = block
    lanes, rows = iota(real.shape, 1), iota(real.shape, 0)
    cols = columns(block, first, group)
    for k in range(group):
        col_real, col_imag = cols[k]
        pivot_real, pivot_imag = col_real[k : k + 1], col_imag[k : k + 1]
        scale = 1.0 / (pivot_real * pivot_real + pivot_imag * pivot_imag)
        mine, here = jnp.where(rows == k, 1.0, 0.0), lanes == first + k
        col_real = col_real - mine
        real, imag = jnp.where(here, mine, real), jnp.where(here, 0.0, imag)

        def step(part_real, part_imag):
            row_real, row_imag = part_real[k : k + 1], part_imag[k : k + 1]
            new_real = row_real * pivot_real + row_imag * pivot_imag
            new_imag = row_imag * pivot_real - row_real * pivot_imag
            change_real = col_real * new_real - col_imag * new_imag
            change_imag = col_real * new_imag + col_imag * new_real
            return part_real - change_real * scale, part_imag - change_imag * scale

        for later in range(k + 1, group):
            cols[later] = step(*cols[later])
        real, imag = step(real, imag)
    return [real, imag]


def unit_rows(shape, first):
    return jnp.where(iota(shape, 1) == iota(shape, 0) + first, 1.0, 0.0)


def stored_and_side(block, first):
    lanes = iota(block[0].shape, 1)
    inside = (lanes >= first) & (lanes < first + group)
    stored = [jnp.where(inside, -part, part) for part in block]
    return stored, [stored[0] + unit_rows(stored[0].shape, first), stored[1]]


def six_products(former, latter):
    former = [former[i] for i in (0, 0, 1, 1, 0, 2)]
    latter = [latter[i] for i in (0, 1, 0, 1, 2, 0)]
    return jnp.concatenate(former, 0), jnp.concatenate(latter, 0)


def sweep_inverse(real, imag, between=()):
    width = real.shape[-1]
    count = 2 * group
    parts = {at: [part[at : at + group] for part in (real, imag)] for at in range(0, width, group)}
    for number, first in enumerate(range(0, width, count)):
        a, b = first, first + group
        olds = jnp.concatenate([parts[at][c] for c in range(2) for at in (a, b)], 0)
        ahead = [at for at in range(first + count, first + count + group * groups_ahead, group) if at < width]
        ahead_cols = [columns(parts[at], first, count) for at in ahead]
        cross = columns(parts[b], a, group)
        stored_a, side_a = stored_and_side(sweep_group(parts[a], a), a)
        block_b = take_away(parts[b], cross, side_a)
        cross = columns(stored_a, b, group)
        stored_b, side_b = stored_and_side(sweep_group(block_b, b), b)
        stored_a = take_away(stored_a, cross, side_b)
        parts[a], parts[b] = stored_a, stored_b
        side_real, side_imag = (jnp.concatenate(pair, 0) for pair in zip(stored_a, stored_b))
        side_real = side_real + unit_rows(side_real.shape, first)
        for at, cols in zip(ahead, ahead_cols):
            parts[at] = take_away(parts[at], cols, [side_real, side_imag])
        sides = [
            jnp.concatenate([jnp.concatenate([r, i], 1), jnp.concatenate([-i, r], 1)], 0)
            for r, i in zip(three_parts(side_real), three_parts(side_imag))
        ]
        change = bf16_dot(*six_products(three_parts(olds), sides), ((0,), (0,)))
        for at in parts:
            if at not in (a, b, *ahead):
                rows = slice(at, at + group)
                parts[at] = [
                    parts[at][0] - change[rows, :width],
                    parts[at][1] - change[rows, width:],
                ]
        if number in between:
            between[number]()
    return [jnp.concatenate([parts[at][c] for at in parts], 0) for c in range(2)]


def column_of(row, unit):
    return jnp.sum(jnp.where(unit, row, 0.0), 1, keepdims=True)


def moved(real, imag, places, turned):
    rows = real.shape[0]
    both = jnp.concatenate(three_parts(jnp.concatenate([real, imag], 0)), 1)
    both = bf16_dot(both, jnp.concatenate([places] * 3, 0), ((1,), (0,)))
    both = jnp.concatenate([both[:rows], both[rows:]], 1)
    both = jnp.concatenate(three_parts(both), 0)
    both = bf16_dot(jnp.concatenate([turned] * 3, 1), both, ((1,), (0,)))
    return both[:, :rows], both[:, rows:]


def form_block(ham, sigma, rate, broad, coupling, slab, energy):
    width = ham.shape[-1]
    unit = iota((width, width), 0) == iota((width, width), 1)
    total = ham + sigma
    real = jnp.where(unit, energy, 0.0) - 0.5 * (total + total.T)
    return real, broad + rate + jnp.where(slab == 0, coupling * coupling, 0.0)


def pair_maps(row, perm, slab):
    width = row.shape[-1]
    rows, lanes = iota((width, width), 0), iota((width, width), 1)
    unit = rows == lanes
    by_column = rows.astype(jnp.float32) == perm
    by_row = lanes.astype(jnp.float32) == column_of(perm, unit)
    col = column_of(row, ((slab == 1) & by_column) | ((slab == 0) & unit))
    scale = col * jnp.sum(jnp.where(unit, col, 0.0), 0, keepdims=True)
    places = jnp.where(((slab == 1) & by_column) | ((slab == 0) & by_row), 1.0, 0.0)
    turned = jnp.where(((slab == 1) & by_row) | ((slab == 0) & by_column), 1.0, 0.0)
    return scale, places.astype(jnp.bfloat16), turned.astype(jnp.bfloat16)


def energy_of(total):
    return -2.0 + 4.0 * lax.axis_index("energy").astype(jnp.float32) / (total - 1)


def splat_kernel(splats, offsets, weights, occupied, total):
    shape = splats.shape[1:]
    spread = (iota(shape, 1) - (total - 1)).astype(jnp.float32)
    modes = offsets.shape[0]
    value = jnp.zeros(shape, jnp.float32)
    for mode in range(modes):
        shift = offsets[mode].astype(jnp.float32)
        strength = weights[mode].astype(jnp.float32)
        value += strength * (occupied[mode] + 1.0) * lorentz(spread - shift, float(total))
        value += strength * occupied[mode] * lorentz(spread + shift, float(total))
    value = value * (-phonon_scale / modes)
    for i in range(splats.shape[0]):
        splats[i] = jnp.broadcast_to(value[:, i : i + 1], shape)


def packed_rows(part):
    half = part.shape[0] // 2
    lanes, rows = iota((half, 2 * half), 1), iota((half, 2 * half), 0)
    lower = part[half:]
    packed = jnp.where(lanes < rows, pltpu.roll(lower, half, 1), part[:half])
    return packed, jnp.sum(jnp.where(lanes == rows + half, lower, 0.0), 0, keepdims=True)


def unpacked(packed, diagonal):
    half = packed.shape[0]
    lanes, rows = iota(packed.shape, 1), iota(packed.shape, 0)
    turned = jnp.concatenate([packed, jnp.zeros_like(packed)], 0).T
    upper = jnp.where(lanes >= rows, packed, turned[:half])
    corner = pltpu.roll(jnp.where(lanes < rows, packed, turned[:half]), half, 1)
    corner = jnp.where(lanes == rows + half, diagonal, corner)
    return upper, jnp.where(lanes < half, turned[half:], corner)


def pair_kernel(
    total,
    *refs,
):
    inputs, broad, green, fresh = refs[:8], *refs[8:11]
    pair_step_on_device(total, inputs, refs[11:19], broad, green, fresh, *refs[19:])


def pair_step_on_device(
    total,
    inputs,
    held,
    broad,
    green,
    fresh,
    input_sems,
    raw,
    theirs,
    scale,
    places,
    turned,
    negated,
    given,
    packed,
    rest,
    landed,
    rests,
    mixed,
    home,
    splats,
    pair_sems,
    away_sems,
    rest_sems,
    back_sems,
):
    fetches = [
        pltpu.make_async_copy(source, target, input_sems.at[i])
        for i, (source, target) in enumerate(zip(inputs, held))
    ]
    for fetch in fetches:
        fetch.start()
    ham, sigma, rate, coupling, perm, offsets, weights, occupied = held
    slab, me = lax.axis_index("slab"), lax.axis_index("energy")
    width = ham.shape[-1]
    half = width // 2
    rows = landed.shape[2]
    owner = slab == 1

    def across(step):
        peer = me
        bit = 1
        while bit < total:
            if step & bit:
                peer += jnp.where(lax.rem(me // bit, 2) == 0, bit, -bit)
            bit *= 2
        return peer

    peers = [across(step) for step in range(total)]
    barrier = pltpu.get_barrier_semaphore()

    def greet(step, core):
        target = {"energy": peers[step], "slab": core}
        pl.semaphore_signal(barrier, inc=1, device_id=target, device_id_type=MESH)

    for step in range(1, total):
        greet(step, 1)

    @pl.when(slab == 0)
    def _():
        greet(0, 1)

    @pl.when(owner)
    def _():
        for step in range(total):
            greet(step, 0)

    for fetch in fetches:
        fetch.wait()
    real, damping = form_block(
        ham[0], sigma[0, 0], rate[0], broad[0], coupling[...], slab, energy_of(total)
    )
    raw[:width] = real
    row = iota((8, width), 0)
    raw[width:] = jnp.where(
        row == 0, damping, jnp.where(row == 1, coupling[...], perm[...].astype(jnp.float32))
    )
    partner = {"slab": 1 - slab}
    swap = pltpu.make_async_remote_copy(
        raw, theirs, pair_sems.at[0], pair_sems.at[1], partner, MESH
    )

    def open_swap():
        @pl.when(slab == 0)
        def _():
            pl.semaphore_wait(barrier, total)

        @pl.when(owner)
        def _():
            pl.semaphore_wait(barrier, 2 * total - 1)

        swap.start()

    def close_swap():
        swap.wait_recv()
        row, order = (
            jnp.where(owner, raw[width + i : width + i + 1], theirs[width + i : width + i + 1])
            for i in (1, 2)
        )
        scale[...], places[...], turned[...] = pair_maps(row, order, slab)

    unit = iota((width, width), 0) == iota((width, width), 1)
    splat_kernel(splats, offsets, weights, occupied, total)
    real, imag = sweep_inverse(
        real, jnp.where(unit, damping, 0.0), {2: open_swap, 6: close_swap}
    )
    real, imag = moved(real * scale[...], imag * scale[...], places[...], turned[...])
    real, imag = sweep_inverse(
        theirs[:width] + real, jnp.where(unit, theirs[width : width + 1], 0.0) + imag
    )

    spare = []
    for part, value in enumerate((real, imag)):
        packed[part * half : (part + 1) * half], diagonal = packed_rows(value)
        spare.append(diagonal)
    rest[...] = spare[0] + pltpu.roll(jnp.broadcast_to(spare[1], (8, width)), half, 1)[:1]
    negated[0] = -real
    negated[1] = -imag

    def away(step):
        return pltpu.make_async_remote_copy(
            packed.at[pl.ds(peers[step] * rows, rows)],
            landed.at[slab, me],
            away_sems.at[0],
            away_sems.at[1],
            {"energy": peers[step], "slab": 1},
            MESH,
        )

    def rest_away(step):
        return pltpu.make_async_remote_copy(
            rest,
            rests.at[me],
            rest_sems.at[0],
            rest_sems.at[1],
            {"energy": peers[step], "slab": 1 - slab},
            MESH,
        )

    hand = pltpu.make_async_remote_copy(
        negated, given, pair_sems.at[2], pair_sems.at[3], partner, MESH
    )

    def back(e, part):
        return pltpu.make_async_remote_copy(
            mixed.at[part, e],
            home.at[pl.ds(me * rows, rows)],
            back_sems.at[0],
            back_sems.at[1],
            {"energy": e, "slab": 1 - part},
            MESH,
        )

    def whole(ref, count, sems):
        part = ref.at[pl.ds(0, count)]
        return pltpu.make_async_remote_copy(part, part, sems.at[0], sems.at[1], partner, MESH)

    own_rows = pl.ds(pl.multiple_of(me * rows, rows), rows)
    for step in range(total - 1, 0, -1):
        away(step).start()

    @pl.when(slab == 0)
    def _():
        away(0).start()

    hand.start()
    for step in range(total - 1, -1, -1):
        rest_away(step).start()

    @pl.when(owner)
    def _():
        landed[slab, me] = packed[own_rows, :]
        flat = (2 * total - 1) * rows
        wide = mixed.reshape(2 * total * rows, width)
        whole(wide, flat, away_sems).wait_recv()
        every = [landed[part] for part in range(2)]
        for e in range(total):
            factors = splats[total - 1 - e : 2 * total - 1 - e]
            for part in range(1, -1, -1):
                mixed[part, e] = jnp.sum(factors * every[part], 0)
            back(e, 1).start()

            @pl.when(me != e)
            def _():
                back(e, 0).start()

        home[own_rows, :] = mixed[0, me]

    hand.wait_recv()
    green[...] = given[...].reshape(2 * width, width)
    rest_all = pltpu.make_async_remote_copy(
        rests, rests, rest_sems.at[0], rest_sems.at[1], partner, MESH
    )
    rest_all.wait_recv()
    spare = jnp.zeros((1, width), jnp.float32)
    for f in range(total):
        spare += splats[f - me + total - 1, :1, :] * rests[f]
    fresh[width:] = jnp.broadcast_to(spare, (8, width))
    swap.wait_send()
    hand.wait_send()
    rest_all.wait_send()

    @pl.when(slab == 0)
    def _():
        whole(packed, width, away_sems).wait_send()
        whole(home, width, back_sems).wait_recv()

    @pl.when(owner)
    def _():
        whole(packed, width - rows, away_sems).wait_send()
        whole(home, width - rows, back_sems).wait_recv()
        flat = (2 * total - 1) * rows
        wide = mixed.reshape(2 * total * rows, width)
        whole(wide, flat, back_sems).wait_send()

    fresh[:width] = home[...]


def closing_kernel(green, fresh, green_out, fresh_out, unfolded, sems):
    width = fresh.shape[-1]
    half = width // 2
    first = pltpu.make_async_copy(green, green_out, sems.at[0])
    first.start()
    spare = fresh[width : width + 1]
    spare = [spare, pltpu.roll(jnp.broadcast_to(spare, (8, width)), half, 1)[:1]]
    for part in range(2):
        upper, lower = unpacked(fresh[part * half : (part + 1) * half, :], spare[part])
        unfolded[part * width : part * width + half, :] = upper
        unfolded[part * width + half : (part + 1) * width, :] = lower
    second = pltpu.make_async_copy(unfolded, fresh_out, sems.at[1])
    second.start()
    first.wait()
    second.wait()


def inverse_kernel(block, out):
    real, imag = sweep_inverse(block[0, 0], block[0, 1])
    out[0, 0] = -real
    out[0, 1] = -imag


def complex_inverse(block):
    count, _, width, _ = block.shape
    spec = pl.BlockSpec((1, 2, width, width), lambda i: (i, 0, 0, 0))
    return pl.pallas_call(
        inverse_kernel,
        grid=(count,),
        out_shape=jax.ShapeDtypeStruct(block.shape, jnp.float32),
        in_specs=[spec],
        out_specs=spec,
    )(block)


def passed_along(block, axis, distance):
    devices = range(lax.axis_size(axis))
    route = [(i - distance, i) for i in devices if i - distance in devices]
    return lax.ppermute(block, axis, route)


def left_apply(matrix, block):
    return jnp.einsum("ij,ecjk->ecik", matrix, block, precision=exact_dots)


def right_apply(block, matrix):
    return jnp.einsum("ecij,jk->ecik", block, matrix, precision=exact_dots)


def inward(coupled, block):
    return left_apply(coupled.T, right_apply(block, coupled))


def outward(coupled, block):
    return left_apply(coupled, right_apply(block, coupled.T))


def paired_inverse(first, second):
    count = first.shape[0]
    both = complex_inverse(jnp.concatenate([first, second], 0))
    return (both[:count], both[count:])


def lorentz(offset, total):
    return 1.0 / (1.0 + (16.0 * offset / total) ** 2)


def kernel_rows(row_energy, col_energy, offsets, weights, occupied, total):
    spread = col_energy[None, :, None] - row_energy[:, None, None]
    shifts = offsets.astype(jnp.float32)
    strength = weights.astype(jnp.float32)
    terms = strength * (occupied + 1.0) * lorentz(
        spread - shifts, total
    ) + strength * occupied * lorentz(spread + shifts, total)
    return jnp.sum(terms, -1) / offsets.shape[0]


def swept_green(hamiltonian, sigma_real, scatter_rate, broadening, coupling, coupling_perm):
    energy_count = broadening.shape[0]
    width = hamiltonian.shape[-1]
    slab_count = lax.axis_size("slab")
    total = energy_count * lax.axis_size("energy")
    slab_pos = lax.axis_index("slab")
    energy_ids = lax.axis_index("energy") * energy_count + jnp.arange(energy_count, dtype=jnp.int32)
    energy = -2.0 + 4.0 * energy_ids.astype(jnp.float32) / (total - 1)
    identity_matrix = jnp.eye(width, dtype=jnp.float32)
    symmetric = 0.5 * (hamiltonian[0] + hamiltonian[0].T)
    real_self = sigma_real[:, 0]
    real_self = 0.5 * (real_self + jnp.swapaxes(real_self, -1, -2))
    lead_rate = jnp.where(slab_pos == 0, coupling[0] ** 2, 0.0)
    damping = broadening[:, None] + scatter_rate[:, 0] + lead_rate[None, :]
    real_block = energy[:, None, None] * identity_matrix - symmetric - real_self
    imag_block = damping[:, :, None] * identity_matrix
    blocks = jnp.stack([real_block, imag_block], 1)
    columns = jnp.arange(width, dtype=jnp.int32)
    coupled = coupling[0][:, None] * (coupling_perm[0][:, None] == columns[None, :]).astype(
        jnp.float32
    )
    left_green = right_green = complex_inverse(blocks)
    from_left = jnp.zeros_like(blocks)
    from_right = jnp.zeros_like(blocks)
    for sweep_num in range(slab_count - 1):
        received = passed_along(left_green, "slab", 1)
        from_right = passed_along(outward(coupled, right_green), "slab", -1)
        from_left = inward(coupled, received)
        if sweep_num < slab_count - 2:
            left_green, right_green = paired_inverse(blocks - from_left, blocks - from_right)
    return complex_inverse(blocks - from_left - from_right)


def pair_step(
    hamiltonian,
    sigma_real,
    scatter_rate,
    broadening,
    coupling,
    coupling_perm,
    mode_offset,
    mode_weight,
    occupation,
):
    width = hamiltonian.shape[-1]
    total = lax.axis_size("energy")
    rows = width // total
    flat = jax.ShapeDtypeStruct((2 * width, width), jnp.float32)
    folded = jax.ShapeDtypeStruct((width + 8, width), jnp.float32)
    complex_block = pltpu.VMEM((2, width, width), jnp.float32)
    with_rows = pltpu.VMEM((width + 8, width), jnp.float32)
    square = pltpu.VMEM((width, width), jnp.float32)
    small_square = pltpu.VMEM((width, width), jnp.bfloat16)
    dma = pltpu.SemaphoreType.DMA
    arrays = (
        hamiltonian,
        sigma_real,
        scatter_rate[0],
        coupling,
        coupling_perm,
        mode_offset,
        mode_weight,
        occupation,
    )
    green, fresh = pl.pallas_call(
        functools.partial(pair_kernel, total),
        out_shape=(flat, folded),
        in_specs=[pl.BlockSpec(memory_space=pl.ANY)] * 8 + [SMEM],
        out_specs=(VMEM, VMEM),
        scratch_shapes=[pltpu.VMEM(array.shape, array.dtype) for array in arrays[:5]]
        + [pltpu.SMEM(array.shape, array.dtype) for array in arrays[5:]]
        + [
            dma((8,)),
            with_rows,
            with_rows,
            square,
            small_square,
            small_square,
            complex_block,
            complex_block,
            square,
            pltpu.VMEM((1, width), jnp.float32),
            pltpu.VMEM((2, total, rows, width), jnp.float32),
            pltpu.VMEM((total, 1, width), jnp.float32),
            pltpu.VMEM((2, total, rows, width), jnp.float32),
            square,
            pltpu.VMEM((2 * total - 1, 8, width), jnp.float32),
            dma((4,)),
            dma((2,)),
            dma((2,)),
            dma((2,)),
        ],
        compiler_params=pltpu.CompilerParams(
            collective_id=0, has_side_effects=True, vmem_limit_bytes=kernel_bytes
        ),
    )(*[pltpu.with_memory_space_constraint(array, pltpu.HBM) for array in arrays], broadening)
    anywhere = pl.BlockSpec(memory_space=pl.ANY)
    green, fresh = pl.pallas_call(
        closing_kernel,
        out_shape=(flat, flat),
        in_specs=[VMEM, VMEM],
        out_specs=(anywhere, anywhere),
        scratch_shapes=[pltpu.VMEM((2 * width, width), jnp.float32), dma((2,))],
        compiler_params=pltpu.CompilerParams(vmem_limit_bytes=kernel_bytes),
    )(green, fresh)
    shape = (1, 1, 2, width, width)
    return green.reshape(shape), fresh.reshape(shape)


def shards(
    hamiltonian,
    sigma_real,
    scatter_rate,
    broadening,
    coupling,
    coupling_perm,
    mode_offset,
    mode_weight,
    occupation,
):
    energy_count = broadening.shape[0]
    width = hamiltonian.shape[-1]
    total = energy_count * lax.axis_size("energy")
    grouped = total & (total - 1) == 0 and width == 8 * total
    if lax.axis_size("slab") == 2 and energy_count == 1 and grouped:
        return pair_step(
            hamiltonian,
            sigma_real,
            scatter_rate,
            broadening,
            coupling,
            coupling_perm,
            mode_offset,
            mode_weight,
            occupation,
        )
    green_diag = swept_green(
        hamiltonian, sigma_real, scatter_rate, broadening, coupling, coupling_perm
    )
    whole_grid = jnp.arange(total, dtype=jnp.float32)
    full_kernel = kernel_rows(
        whole_grid, whole_grid, mode_offset, mode_weight, occupation, float(total)
    )
    flat_rows = green_diag.reshape(energy_count, 2 * width, width)
    mixed = jnp.einsum(
        "ef,frc->erc",
        full_kernel,
        lax.all_to_all(flat_rows, "energy", split_axis=1, concat_axis=0, tiled=True),
        precision=exact_dots,
    )
    summed = lax.all_to_all(mixed, "energy", split_axis=0, concat_axis=1, tiled=True)
    summed = summed.reshape(energy_count, 2, width, width)
    sigma_new = phonon_scale * summed
    return (green_diag[:, None], sigma_new[:, None])


def solution(mesh):
    in_specs = (
        P("slab", None, None),
        P("energy", "slab", None, None),
        P("energy", "slab", None),
        P("energy"),
        P("slab", None),
        P("slab", None),
        P(),
        P(),
        P(),
    )
    out_specs = (P("energy", "slab", None, None, None), P("energy", "slab", None, None, None))
    return jax.shard_map(shards, mesh=mesh, in_specs=in_specs, out_specs=out_specs, check_vma=False)
```

```python
import functools

import jax
import jax.numpy as jnp
from jax import lax
from jax.experimental import pallas as pl
from jax.experimental.pallas import tpu as pltpu
from jax.sharding import PartitionSpec as P

exact_dots = lax.Precision.HIGHEST
phonon_scale = 0.01
group = 8
groups_ahead = 1
kernel_bytes = 8 * 2**20
VMEM = pl.BlockSpec(memory_space=pltpu.VMEM)
MESH = pl.DeviceIdType.MESH
SMEM = pl.BlockSpec(memory_space=pltpu.SMEM)


def iota(shape, dim):
    return lax.broadcasted_iota(jnp.int32, shape, dim)


def three_parts(value):
    high = value.astype(jnp.bfloat16)
    rest = value - high.astype(jnp.float32)
    middle = rest.astype(jnp.bfloat16)
    low = (rest - middle.astype(jnp.float32)).astype(jnp.bfloat16)
    return high, middle, low


def bf16_dot(former, latter, contract):
    return lax.dot_general(
        former, latter, (contract, ((), ())), preferred_element_type=jnp.float32
    )


def spread(part, lane):
    return jnp.broadcast_to(part[:, lane : lane + 1], part.shape)


def columns(block, first, count):
    return [[spread(part, first + k) for part in block] for k in range(count)]


def tree_sum(terms):
    while len(terms) > 1:
        terms = [a + b for a, b in zip(terms[::2], terms[1::2])]
    return terms[0]


def take_away(block, cols, rows):
    reals, imags = [], []
    for k, (col_real, col_imag) in enumerate(cols):
        row_real, row_imag = rows[0][k : k + 1], rows[1][k : k + 1]
        reals.append(col_real * row_real - col_imag * row_imag)
        imags.append(col_real * row_imag + col_imag * row_real)
    return [block[0] - tree_sum(reals), block[1] - tree_sum(imags)]


def sweep_group(block, first):
    real, imag = block
    lanes, rows = iota(real.shape, 1), iota(real.shape, 0)
    cols = columns(block, first, group)
    for k in range(group):
        col_real, col_imag = cols[k]
        pivot_real, pivot_imag = col_real[k : k + 1], col_imag[k : k + 1]
        scale = 1.0 / (pivot_real * pivot_real + pivot_imag * pivot_imag)
        mine, here = jnp.where(rows == k, 1.0, 0.0), lanes == first + k
        col_real = col_real - mine
        real, imag = jnp.where(here, mine, real), jnp.where(here, 0.0, imag)

        def step(part_real, part_imag):
            row_real, row_imag = part_real[k : k + 1], part_imag[k : k + 1]
            new_real = row_real * pivot_real + row_imag * pivot_imag
            new_imag = row_imag * pivot_real - row_real * pivot_imag
            change_real = col_real * new_real - col_imag * new_imag
            change_imag = col_real * new_imag + col_imag * new_real
            return part_real - change_real * scale, part_imag - change_imag * scale

        for later in range(k + 1, group):
            cols[later] = step(*cols[later])
        real, imag = step(real, imag)
    return [real, imag]


def unit_rows(shape, first):
    return jnp.where(iota(shape, 1) == iota(shape, 0) + first, 1.0, 0.0)


def stored_and_side(block, first):
    lanes = iota(block[0].shape, 1)
    inside = (lanes >= first) & (lanes < first + group)
    stored = [jnp.where(inside, -part, part) for part in block]
    return stored, [stored[0] + unit_rows(stored[0].shape, first), stored[1]]


def six_products(former, latter):
    former = [former[i] for i in (0, 0, 1, 1, 0, 2)]
    latter = [latter[i] for i in (0, 1, 0, 1, 2, 0)]
    return jnp.concatenate(former, 0), jnp.concatenate(latter, 0)


def sweep_inverse(real, imag, between=()):
    width = real.shape[-1]
    count = 2 * group
    parts = {at: [part[at : at + group] for part in (real, imag)] for at in range(0, width, group)}
    for number, first in enumerate(range(0, width, count)):
        a, b = first, first + group
        olds = jnp.concatenate([parts[at][c] for c in range(2) for at in (a, b)], 0)
        ahead = [at for at in range(first + count, first + count + group * groups_ahead, group) if at < width]
        ahead_cols = [columns(parts[at], first, count) for at in ahead]
        cross = columns(parts[b], a, group)
        stored_a, side_a = stored_and_side(sweep_group(parts[a], a), a)
        block_b = take_away(parts[b], cross, side_a)
        cross = columns(stored_a, b, group)
        stored_b, side_b = stored_and_side(sweep_group(block_b, b), b)
        stored_a = take_away(stored_a, cross, side_b)
        parts[a], parts[b] = stored_a, stored_b
        side_real, side_imag = (jnp.concatenate(pair, 0) for pair in zip(stored_a, stored_b))
        side_real = side_real + unit_rows(side_real.shape, first)
        for at, cols in zip(ahead, ahead_cols):
            parts[at] = take_away(parts[at], cols, [side_real, side_imag])
        sides = [
            jnp.concatenate([jnp.concatenate([r, i], 1), jnp.concatenate([-i, r], 1)], 0)
            for r, i in zip(three_parts(side_real), three_parts(side_imag))
        ]
        change = bf16_dot(*six_products(three_parts(olds), sides), ((0,), (0,)))
        for at in parts:
            if at not in (a, b, *ahead):
                rows = slice(at, at + group)
                parts[at] = [
                    parts[at][0] - change[rows, :width],
                    parts[at][1] - change[rows, width:],
                ]
        if number in between:
            between[number]()
    return [jnp.concatenate([parts[at][c] for at in parts], 0) for c in range(2)]


def column_of(row, unit):
    return jnp.sum(jnp.where(unit, row, 0.0), 1, keepdims=True)


def moved(real, imag, places, turned):
    rows = real.shape[0]
    both = jnp.concatenate(three_parts(jnp.concatenate([real, imag], 0)), 1)
    both = bf16_dot(both, jnp.concatenate([places] * 3, 0), ((1,), (0,)))
    both = jnp.concatenate([both[:rows], both[rows:]], 1)
    both = jnp.concatenate(three_parts(both), 0)
    both = bf16_dot(jnp.concatenate([turned] * 3, 1), both, ((1,), (0,)))
    return both[:, :rows], both[:, rows:]


def form_block(ham, sigma, rate, broad, coupling, slab, energy):
    width = ham.shape[-1]
    unit = iota((width, width), 0) == iota((width, width), 1)
    total = ham + sigma
    real = jnp.where(unit, energy, 0.0) - 0.5 * (total + total.T)
    return real, broad + rate + jnp.where(slab == 0, coupling * coupling, 0.0)


def pair_maps(row, perm, slab):
    width = row.shape[-1]
    rows, lanes = iota((width, width), 0), iota((width, width), 1)
    unit = rows == lanes
    by_column = rows.astype(jnp.float32) == perm
    by_row = lanes.astype(jnp.float32) == column_of(perm, unit)
    col = column_of(row, ((slab == 1) & by_column) | ((slab == 0) & unit))
    scale = col * jnp.sum(jnp.where(unit, col, 0.0), 0, keepdims=True)
    places = jnp.where(((slab == 1) & by_column) | ((slab == 0) & by_row), 1.0, 0.0)
    turned = jnp.where(((slab == 1) & by_row) | ((slab == 0) & by_column), 1.0, 0.0)
    return scale, places.astype(jnp.bfloat16), turned.astype(jnp.bfloat16)


def energy_of(total):
    return -2.0 + 4.0 * lax.axis_index("energy").astype(jnp.float32) / (total - 1)


def splat_kernel(splats, offsets, weights, occupied, total):
    shape = splats.shape[1:]
    spread = (iota(shape, 1) - (total - 1)).astype(jnp.float32)
    modes = offsets.shape[0]
    value = jnp.zeros(shape, jnp.float32)
    for mode in range(modes):
        shift = offsets[mode].astype(jnp.float32)
        strength = weights[mode].astype(jnp.float32)
        value += strength * (occupied[mode] + 1.0) * lorentz(spread - shift, float(total))
        value += strength * occupied[mode] * lorentz(spread + shift, float(total))
    value = value * (-phonon_scale / modes)
    for i in range(splats.shape[0]):
        splats[i] = jnp.broadcast_to(value[:, i : i + 1], shape)


def packed_rows(part):
    half = part.shape[0] // 2
    lanes, rows = iota((half, 2 * half), 1), iota((half, 2 * half), 0)
    lower = part[half:]
    packed = jnp.where(lanes < rows, pltpu.roll(lower, half, 1), part[:half])
    return packed, jnp.sum(jnp.where(lanes == rows + half, lower, 0.0), 0, keepdims=True)


def unpacked(packed, diagonal):
    half = packed.shape[0]
    lanes, rows = iota(packed.shape, 1), iota(packed.shape, 0)
    turned = jnp.concatenate([packed, jnp.zeros_like(packed)], 0).T
    upper = jnp.where(lanes >= rows, packed, turned[:half])
    corner = pltpu.roll(jnp.where(lanes < rows, packed, turned[:half]), half, 1)
    corner = jnp.where(lanes == rows + half, diagonal, corner)
    return upper, jnp.where(lanes < half, turned[half:], corner)


def pair_kernel(
    total,
    *refs,
):
    inputs, broad, green, fresh = refs[:8], *refs[8:11]
    pair_step_on_device(total, inputs, refs[11:19], broad, green, fresh, *refs[19:])


def pair_step_on_device(
    total,
    inputs,
    held,
    broad,
    green,
    fresh,
    input_sems,
    raw,
    theirs,
    scale,
    places,
    turned,
    negated,
    given,
    packed,
    rest,
    landed,
    rests,
    mixed,
    home,
    splats,
    pair_sems,
    away_sems,
    rest_sems,
    back_sems,
):
    fetches = [
        pltpu.make_async_copy(source, target, input_sems.at[i])
        for i, (source, target) in enumerate(zip(inputs, held))
    ]
    for fetch in fetches:
        fetch.start()
    ham, sigma, rate, coupling, perm, offsets, weights, occupied = held
    slab, me = lax.axis_index("slab"), lax.axis_index("energy")
    width = ham.shape[-1]
    half = width // 2
    rows = landed.shape[2]
    owner = slab == 1

    def across(step):
        peer = me
        bit = 1
        while bit < total:
            if step & bit:
                peer += jnp.where(lax.rem(me // bit, 2) == 0, bit, -bit)
            bit *= 2
        return peer

    peers = [across(step) for step in range(total)]
    barrier = pltpu.get_barrier_semaphore()

    def greet(step, core):
        target = {"energy": peers[step], "slab": core}
        pl.semaphore_signal(barrier, inc=1, device_id=target, device_id_type=MESH)

    for step in range(1, total):
        greet(step, 1)

    @pl.when(slab == 0)
    def _():
        greet(0, 1)

    @pl.when(owner)
    def _():
        for step in range(total):
            greet(step, 0)

    for fetch in fetches:
        fetch.wait()
    real, damping = form_block(
        ham[0], sigma[0, 0], rate[0], broad[0], coupling[...], slab, energy_of(total)
    )
    raw[:width] = real
    row = iota((8, width), 0)
    raw[width:] = jnp.where(
        row == 0, damping, jnp.where(row == 1, coupling[...], perm[...].astype(jnp.float32))
    )
    partner = {"slab": 1 - slab}
    swap = pltpu.make_async_remote_copy(
        raw, theirs, pair_sems.at[0], pair_sems.at[1], partner, MESH
    )

    def open_swap():
        @pl.when(slab == 0)
        def _():
            pl.semaphore_wait(barrier, total)

        @pl.when(owner)
        def _():
            pl.semaphore_wait(barrier, 2 * total - 1)

        swap.start()

    def close_swap():
        swap.wait_recv()
        row, order = (
            jnp.where(owner, raw[width + i : width + i + 1], theirs[width + i : width + i + 1])
            for i in (1, 2)
        )
        scale[...], places[...], turned[...] = pair_maps(row, order, slab)

    unit = iota((width, width), 0) == iota((width, width), 1)
    splat_kernel(splats, offsets, weights, occupied, total)
    real, imag = sweep_inverse(
        real, jnp.where(unit, damping, 0.0), {5: open_swap, 7: close_swap}
    )
    real, imag = moved(real * scale[...], imag * scale[...], places[...], turned[...])
    real, imag = sweep_inverse(
        theirs[:width] + real, jnp.where(unit, theirs[width : width + 1], 0.0) + imag
    )

    spare = []
    for part, value in enumerate((real, imag)):
        packed[part * half : (part + 1) * half], diagonal = packed_rows(value)
        spare.append(diagonal)
    rest[...] = spare[0] + pltpu.roll(jnp.broadcast_to(spare[1], (8, width)), half, 1)[:1]
    negated[0] = -real
    negated[1] = -imag

    def away(step):
        return pltpu.make_async_remote_copy(
            packed.at[pl.ds(peers[step] * rows, rows)],
            landed.at[slab, me],
            away_sems.at[0],
            away_sems.at[1],
            {"energy": peers[step], "slab": 1},
            MESH,
        )

    def rest_away(step):
        return pltpu.make_async_remote_copy(
            rest,
            rests.at[me],
            rest_sems.at[0],
            rest_sems.at[1],
            {"energy": peers[step], "slab": 1 - slab},
            MESH,
        )

    hand = pltpu.make_async_remote_copy(
        negated, given, pair_sems.at[2], pair_sems.at[3], partner, MESH
    )

    def back(e, part):
        return pltpu.make_async_remote_copy(
            mixed.at[part, e],
            home.at[pl.ds(me * rows, rows)],
            back_sems.at[0],
            back_sems.at[1],
            {"energy": e, "slab": 1 - part},
            MESH,
        )

    def whole(ref, count, sems):
        part = ref.at[pl.ds(0, count)]
        return pltpu.make_async_remote_copy(part, part, sems.at[0], sems.at[1], partner, MESH)

    own_rows = pl.ds(pl.multiple_of(me * rows, rows), rows)
    for step in range(total - 1, 0, -1):
        away(step).start()

    @pl.when(slab == 0)
    def _():
        away(0).start()

    hand.start()
    for step in range(total - 1, -1, -1):
        rest_away(step).start()

    @pl.when(owner)
    def _():
        landed[slab, me] = packed[own_rows, :]
        flat = (2 * total - 1) * rows
        wide = mixed.reshape(2 * total * rows, width)
        whole(wide, flat, away_sems).wait_recv()
        every = [landed[part] for part in range(2)]
        for e in range(total):
            factors = splats[total - 1 - e : 2 * total - 1 - e]
            for part in range(1, -1, -1):
                mixed[part, e] = jnp.sum(factors * every[part], 0)
            back(e, 1).start()

            @pl.when(me != e)
            def _():
                back(e, 0).start()

        home[own_rows, :] = mixed[0, me]

    hand.wait_recv()
    green[...] = given[...].reshape(2 * width, width)
    rest_all = pltpu.make_async_remote_copy(
        rests, rests, rest_sems.at[0], rest_sems.at[1], partner, MESH
    )
    rest_all.wait_recv()
    spare = jnp.zeros((1, width), jnp.float32)
    for f in range(total):
        spare += splats[f - me + total - 1, :1, :] * rests[f]
    fresh[width:] = jnp.broadcast_to(spare, (8, width))
    swap.wait_send()
    hand.wait_send()
    rest_all.wait_send()

    @pl.when(slab == 0)
    def _():
        whole(packed, width, away_sems).wait_send()
        whole(home, width, back_sems).wait_recv()

    @pl.when(owner)
    def _():
        whole(packed, width - rows, away_sems).wait_send()
        whole(home, width - rows, back_sems).wait_recv()
        flat = (2 * total - 1) * rows
        wide = mixed.reshape(2 * total * rows, width)
        whole(wide, flat, back_sems).wait_send()

    fresh[:width] = home[...]


def closing_kernel(green, fresh, green_out, fresh_out, unfolded, sems):
    width = fresh.shape[-1]
    half = width // 2
    first = pltpu.make_async_copy(green, green_out, sems.at[0])
    first.start()
    spare = fresh[width : width + 1]
    spare = [spare, pltpu.roll(jnp.broadcast_to(spare, (8, width)), half, 1)[:1]]
    for part in range(2):
        upper, lower = unpacked(fresh[part * half : (part + 1) * half, :], spare[part])
        unfolded[part * width : part * width + half, :] = upper
        unfolded[part * width + half : (part + 1) * width, :] = lower
    second = pltpu.make_async_copy(unfolded, fresh_out, sems.at[1])
    second.start()
    first.wait()
    second.wait()


def inverse_kernel(block, out):
    real, imag = sweep_inverse(block[0, 0], block[0, 1])
    out[0, 0] = -real
    out[0, 1] = -imag


def complex_inverse(block):
    count, _, width, _ = block.shape
    spec = pl.BlockSpec((1, 2, width, width), lambda i: (i, 0, 0, 0))
    return pl.pallas_call(
        inverse_kernel,
        grid=(count,),
        out_shape=jax.ShapeDtypeStruct(block.shape, jnp.float32),
        in_specs=[spec],
        out_specs=spec,
    )(block)


def passed_along(block, axis, distance):
    devices = range(lax.axis_size(axis))
    route = [(i - distance, i) for i in devices if i - distance in devices]
    return lax.ppermute(block, axis, route)


def left_apply(matrix, block):
    return jnp.einsum("ij,ecjk->ecik", matrix, block, precision=exact_dots)


def right_apply(block, matrix):
    return jnp.einsum("ecij,jk->ecik", block, matrix, precision=exact_dots)


def inward(coupled, block):
    return left_apply(coupled.T, right_apply(block, coupled))


def outward(coupled, block):
    return left_apply(coupled, right_apply(block, coupled.T))


def paired_inverse(first, second):
    count = first.shape[0]
    both = complex_inverse(jnp.concatenate([first, second], 0))
    return (both[:count], both[count:])


def lorentz(offset, total):
    return 1.0 / (1.0 + (16.0 * offset / total) ** 2)


def kernel_rows(row_energy, col_energy, offsets, weights, occupied, total):
    spread = col_energy[None, :, None] - row_energy[:, None, None]
    shifts = offsets.astype(jnp.float32)
    strength = weights.astype(jnp.float32)
    terms = strength * (occupied + 1.0) * lorentz(
        spread - shifts, total
    ) + strength * occupied * lorentz(spread + shifts, total)
    return jnp.sum(terms, -1) / offsets.shape[0]


def swept_green(hamiltonian, sigma_real, scatter_rate, broadening, coupling, coupling_perm):
    energy_count = broadening.shape[0]
    width = hamiltonian.shape[-1]
    slab_count = lax.axis_size("slab")
    total = energy_count * lax.axis_size("energy")
    slab_pos = lax.axis_index("slab")
    energy_ids = lax.axis_index("energy") * energy_count + jnp.arange(energy_count, dtype=jnp.int32)
    energy = -2.0 + 4.0 * energy_ids.astype(jnp.float32) / (total - 1)
    identity_matrix = jnp.eye(width, dtype=jnp.float32)
    symmetric = 0.5 * (hamiltonian[0] + hamiltonian[0].T)
    real_self = sigma_real[:, 0]
    real_self = 0.5 * (real_self + jnp.swapaxes(real_self, -1, -2))
    lead_rate = jnp.where(slab_pos == 0, coupling[0] ** 2, 0.0)
    damping = broadening[:, None] + scatter_rate[:, 0] + lead_rate[None, :]
    real_block = energy[:, None, None] * identity_matrix - symmetric - real_self
    imag_block = damping[:, :, None] * identity_matrix
    blocks = jnp.stack([real_block, imag_block], 1)
    columns = jnp.arange(width, dtype=jnp.int32)
    coupled = coupling[0][:, None] * (coupling_perm[0][:, None] == columns[None, :]).astype(
        jnp.float32
    )
    left_green = right_green = complex_inverse(blocks)
    from_left = jnp.zeros_like(blocks)
    from_right = jnp.zeros_like(blocks)
    for sweep_num in range(slab_count - 1):
        received = passed_along(left_green, "slab", 1)
        from_right = passed_along(outward(coupled, right_green), "slab", -1)
        from_left = inward(coupled, received)
        if sweep_num < slab_count - 2:
            left_green, right_green = paired_inverse(blocks - from_left, blocks - from_right)
    return complex_inverse(blocks - from_left - from_right)


def pair_step(
    hamiltonian,
    sigma_real,
    scatter_rate,
    broadening,
    coupling,
    coupling_perm,
    mode_offset,
    mode_weight,
    occupation,
):
    width = hamiltonian.shape[-1]
    total = lax.axis_size("energy")
    rows = width // total
    flat = jax.ShapeDtypeStruct((2 * width, width), jnp.float32)
    folded = jax.ShapeDtypeStruct((width + 8, width), jnp.float32)
    complex_block = pltpu.VMEM((2, width, width), jnp.float32)
    with_rows = pltpu.VMEM((width + 8, width), jnp.float32)
    square = pltpu.VMEM((width, width), jnp.float32)
    small_square = pltpu.VMEM((width, width), jnp.bfloat16)
    dma = pltpu.SemaphoreType.DMA
    arrays = (
        hamiltonian,
        sigma_real,
        scatter_rate[0],
        coupling,
        coupling_perm,
        mode_offset,
        mode_weight,
        occupation,
    )
    green, fresh = pl.pallas_call(
        functools.partial(pair_kernel, total),
        out_shape=(flat, folded),
        in_specs=[pl.BlockSpec(memory_space=pl.ANY)] * 8 + [SMEM],
        out_specs=(VMEM, VMEM),
        scratch_shapes=[pltpu.VMEM(array.shape, array.dtype) for array in arrays[:5]]
        + [pltpu.SMEM(array.shape, array.dtype) for array in arrays[5:]]
        + [
            dma((8,)),
            with_rows,
            with_rows,
            square,
            small_square,
            small_square,
            complex_block,
            complex_block,
            square,
            pltpu.VMEM((1, width), jnp.float32),
            pltpu.VMEM((2, total, rows, width), jnp.float32),
            pltpu.VMEM((total, 1, width), jnp.float32),
            pltpu.VMEM((2, total, rows, width), jnp.float32),
            square,
            pltpu.VMEM((2 * total - 1, 8, width), jnp.float32),
            dma((4,)),
            dma((2,)),
            dma((2,)),
            dma((2,)),
        ],
        compiler_params=pltpu.CompilerParams(
            collective_id=0, has_side_effects=True, vmem_limit_bytes=kernel_bytes
        ),
    )(*[pltpu.with_memory_space_constraint(array, pltpu.HBM) for array in arrays], broadening)
    anywhere = pl.BlockSpec(memory_space=pl.ANY)
    green, fresh = pl.pallas_call(
        closing_kernel,
        out_shape=(flat, flat),
        in_specs=[VMEM, VMEM],
        out_specs=(anywhere, anywhere),
        scratch_shapes=[pltpu.VMEM((2 * width, width), jnp.float32), dma((2,))],
        compiler_params=pltpu.CompilerParams(vmem_limit_bytes=kernel_bytes),
    )(green, fresh)
    shape = (1, 1, 2, width, width)
    return green.reshape(shape), fresh.reshape(shape)


def shards(
    hamiltonian,
    sigma_real,
    scatter_rate,
    broadening,
    coupling,
    coupling_perm,
    mode_offset,
    mode_weight,
    occupation,
):
    energy_count = broadening.shape[0]
    width = hamiltonian.shape[-1]
    total = energy_count * lax.axis_size("energy")
    grouped = total & (total - 1) == 0 and width == 8 * total
    if lax.axis_size("slab") == 2 and energy_count == 1 and grouped:
        return pair_step(
            hamiltonian,
            sigma_real,
            scatter_rate,
            broadening,
            coupling,
            coupling_perm,
            mode_offset,
            mode_weight,
            occupation,
        )
    green_diag = swept_green(
        hamiltonian, sigma_real, scatter_rate, broadening, coupling, coupling_perm
    )
    whole_grid = jnp.arange(total, dtype=jnp.float32)
    full_kernel = kernel_rows(
        whole_grid, whole_grid, mode_offset, mode_weight, occupation, float(total)
    )
    flat_rows = green_diag.reshape(energy_count, 2 * width, width)
    mixed = jnp.einsum(
        "ef,frc->erc",
        full_kernel,
        lax.all_to_all(flat_rows, "energy", split_axis=1, concat_axis=0, tiled=True),
        precision=exact_dots,
    )
    summed = lax.all_to_all(mixed, "energy", split_axis=0, concat_axis=1, tiled=True)
    summed = summed.reshape(energy_count, 2, width, width)
    sigma_new = phonon_scale * summed
    return (green_diag[:, None], sigma_new[:, None])


def solution(mesh):
    in_specs = (
        P("slab", None, None),
        P("energy", "slab", None, None),
        P("energy", "slab", None),
        P("energy"),
        P("slab", None),
        P("slab", None),
        P(),
        P(),
        P(),
    )
    out_specs = (P("energy", "slab", None, None, None), P("energy", "slab", None, None, None))
    return jax.shard_map(shards, mesh=mesh, in_specs=in_specs, out_specs=out_specs, check_vma=False)
```
